32 devices in a mesh: dp: 16 (over z, y, core), rep: 2 (over x).
Axes of the slice: x: 2, y: 2, z: 4, core: 2. Of those that a mesh axis runs over, the one named last changes fastest.
Arguments:
- inputs: bfloat16 [32, 256, 768], P(('dp', 'rep')), may hold values from -6 to 6
- norm_gain: float32 [768], replicated, may hold values from 0.5 to 1.5
- in_weight: bfloat16 [768, 3352], P('dp'), may hold values from -0.21875 to 0.21875
- conv_weight: float32 [4, 1792], replicated, may hold values from -3 to 3
- conv_bias: float32 [1792], replicated, may hold values from -3 to 3
- dt_bias: float32 [24], replicated, may hold values from -6 to -1
- a_log: float32 [24], replicated, may hold values from -2 to 1.5
- skip_gain: float32 [24], replicated, may hold values from 0.5 to 2
- gate_gain: float32 [1536], replicated, may hold values from 0.5 to 1.5
- out_weight: bfloat16 [1536, 768], P('dp'), may hold values from -0.15625 to 0.15625
- cotangent: bfloat16 [32, 256, 768], P(('dp', 'rep')), may hold values from -6 to 6
Outputs:
- output: bfloat16 [32, 256, 768], P(('dp', 'rep'))
- grad_inputs: bfloat16 [32, 256, 768], P(('dp', 'rep'))
- grad_norm_gain: float32 [768], replicated
- grad_in_weight: float32 [768, 3352], P('dp')
- grad_conv_weight: float32 [4, 1792], replicated
- grad_conv_bias: float32 [1792], replicated
- grad_dt_bias: float32 [24], replicated
- grad_a_log: float32 [24], replicated
- grad_skip_gain: float32 [24], replicated
- grad_gate_gain: float32 [1536], replicated
- grad_out_weight: float32 [1536, 768], P('dp')
The draws below stay inside these ranges and needn't reach their ends.
All inputs are finite; a program needn't handle non-finite values.
Results may differ from the reference program's by a relative error of at most 0.0082.
Values may be sent and summed in bfloat16 or wider, within the bound.
A program may use at most 128 MiB of HBM per device.

```python
import jax
import jax.numpy as jnp
from jax import lax

D = 768
HEADS = 24
CONV = 4
SPAN = 256
SEQ_LEN = 256
D_INNER = 1536
CHANNELS = 1792
PROJ = 3352
SEQS = 32


def spiked(values, rng, source, target, blocks, factor):
    owner, partner = [(jnp.arange(values.shape[dim]) // (values.shape[dim] // blocks)).reshape([-1 if axis == dim else 1 for axis in range(values.ndim)]) for dim in (source, target)]
    chosen = jax.random.permutation(rng, blocks)[partner]
    strong = (owner == chosen) | (owner == (partner + blocks // 2) % blocks)
    return jnp.where(strong, factor * values, values)


def levels(own_key, dims, cuts, least, largest):
    level = 1.0
    for axis_at, parts in cuts:
        draws = jax.random.uniform(jax.random.fold_in(jax.random.fold_in(own_key, 6), axis_at), (parts,), jnp.float32, least / len(cuts), largest / len(cuts))
        level = level * jnp.repeat(jnp.exp(draws), dims[axis_at] // parts).reshape((-1,) + (1,) * (len(dims) - 1 - axis_at))
    return level


def gaussian(own_key, shape, scale, most, pieces=(), kind=jnp.bfloat16):
    values = scale * jax.random.normal(own_key, shape, jnp.float32)
    if pieces:
        values = values * levels(own_key, shape, pieces, -0.22, 0.18)
    return jnp.clip(values, -most, most).astype(kind)


def bell_draw_with(rng, extent, deviation, most, shards, heavy, kind=jnp.bfloat16):
    values = deviation * jax.random.normal(rng, extent, jnp.float32)
    if shards:
        values = values * levels(rng, extent, shards, -0.22, 0.18)
    return jnp.clip(spiked(values, jax.random.fold_in(rng, 3), *heavy), -most, most).astype(kind)


def setup_inputs(seed: int = 0) -> dict:
    streams_of = jax.random.split(jax.random.key(seed), 12)
    return {
        "inputs": bell_draw_with(streams_of[0], (SEQS, SEQ_LEN, D), 1.0, 6.0, ((0, 32),), (0, 2, 32, 2.75)),
        "norm_gain": jnp.clip(1.0 + 0.1 * jax.random.normal(streams_of[1], (D,), jnp.float32), 0.5, 1.5),
        "in_weight": gaussian(streams_of[2], (D, PROJ), D ** -0.5, 0.21875, ((0, 16),)),
        "conv_weight": gaussian(streams_of[3], (CONV, CHANNELS), CONV ** -0.5, 3.0, (), jnp.float32),
        "conv_bias": gaussian(streams_of[4], (CHANNELS,), 0.5, 3.0, (), jnp.float32),
        "dt_bias": jnp.clip(jax.random.uniform(streams_of[5], (HEADS,), jnp.float32, -6.0, -1.0), -6.0, -1.0),
        "a_log": jnp.clip(jax.random.uniform(streams_of[6], (HEADS,), jnp.float32, -2.0, 1.5), -2.0, 1.5),
        "skip_gain": jnp.clip(jax.random.uniform(streams_of[7], (HEADS,), jnp.float32, 0.5, 2.0), 0.5, 2.0),
        "gate_gain": jnp.clip(1.0 + 0.1 * jax.random.normal(streams_of[8], (D_INNER,), jnp.float32), 0.5, 1.5),
        "out_weight": gaussian(streams_of[9], (D_INNER, D), D_INNER ** -0.5, 0.15625, ((0, 16),)),
        "cotangent": gaussian(streams_of[10], (SEQS, SEQ_LEN, D), 1.0, 6.0, ((0, 32),)),
    }


def head_mix(values, step_size, decay_rate, b_blocks, c_blocks, scores):
    length = values.shape[1]
    scaled = step_size * decay_rate
    running = jnp.cumsum(scaled, axis=1)
    row_ids = lax.broadcasted_iota(jnp.int32, (length, length), 0)
    col_ids = lax.broadcasted_iota(jnp.int32, (length, length), 1)
    causal = row_ids >= col_ids
    spread = running[:, :, None] - running[:, None, :]
    decays = jnp.exp(jnp.where(causal[None], spread, -jnp.inf))
    weight = scores * decays * step_size[:, None, :]
    within = jnp.einsum('cqs,csp->cqp', weight, values, precision=lax.Precision.HIGHEST)
    to_end = jnp.exp(running[:, -1:] - running) * step_size
    states = jnp.einsum('cs,csn,csp->cnp', to_end, b_blocks, values, precision=lax.Precision.HIGHEST)
    before = jnp.zeros(states.shape[1:], states.dtype)
    priors = []
    for block_id in range(states.shape[0]):
        priors.append(before)
        before = jnp.exp(running[block_id, -1]) * before + states[block_id]
    carried = jnp.stack(priors)
    across = jnp.einsum('cqn,cnp->cqp', c_blocks, carried, precision=lax.Precision.HIGHEST)
    return within + across * jnp.exp(running)[:, :, None]

def mixer(projected, conv_weight, conv_bias, dt_bias, a_log, skip_gain, gate_gain):
    length = projected.shape[0]
    inner_width = gate_gain.shape[0]
    head_count = skip_gain.shape[0]
    channels = conv_bias.shape[0]
    state_width = (channels - inner_width) // 2
    tap_count = conv_weight.shape[0]
    gate_in = projected[:, :inner_width]
    conv_in = projected[:, inner_width:inner_width + channels]
    step_raw = projected[:, inner_width + channels:]
    padded = jnp.pad(conv_in, ((tap_count - 1, 0), (0, 0)))
    convolved = conv_bias + jnp.zeros_like(conv_in)
    for offset in range(tap_count):
        convolved = convolved + conv_weight[offset] * padded[offset:offset + length]
    active = jax.nn.silu(convolved)
    values = active[:, :inner_width]
    b_proj = active[:, inner_width:inner_width + state_width]
    c_proj = active[:, inner_width + state_width:]
    step_size = jax.nn.softplus(step_raw + dt_bias)
    decay_rate = -jnp.exp(a_log)
    blocks = length // SPAN
    b_blocks = b_proj.reshape(blocks, SPAN, state_width)
    c_blocks = c_proj.reshape(blocks, SPAN, state_width)
    scores = jnp.einsum('cqn,csn->cqs', c_blocks, b_blocks, precision=lax.Precision.HIGHEST)
    head_values = values.reshape(blocks, SPAN, head_count, inner_width // head_count).transpose(2, 0, 1, 3)
    head_steps = step_size.reshape(blocks, SPAN, head_count).transpose(2, 0, 1)

    def one_head(member):
        return head_mix(member[0], member[1], member[2], b_blocks, c_blocks, scores)
    mixed_heads = lax.map(jax.checkpoint(one_head), (head_values, head_steps, decay_rate))
    scanned = mixed_heads.transpose(1, 2, 0, 3).reshape(length, inner_width)
    skipped = values.reshape(length, head_count, inner_width // head_count) * skip_gain[:, None]
    scanned = scanned + skipped.reshape(length, inner_width)
    gated_out = scanned * jax.nn.silu(gate_in)
    return gated_out * lax.rsqrt(lax.optimization_barrier(jnp.mean(gated_out * gated_out, axis=-1, keepdims=True)) + 1e-05) * gate_gain

def front_norm(rows_in, norm_gain):
    return rows_in * lax.rsqrt(lax.optimization_barrier(jnp.mean(rows_in * rows_in, axis=-1, keepdims=True)) + 1e-05) * norm_gain

def reference(inputs, norm_gain, in_weight, conv_weight, conv_bias, dt_bias, a_log, skip_gain, gate_gain, out_weight, cotangent):

    def per_sequence(totals, paired):
        sequence, sequence_grad = paired
        rows_in = sequence.astype(jnp.float32)
        normed, norm_back = jax.vjp(front_norm, rows_in, norm_gain)
        normed_low = normed.astype(jnp.bfloat16)
        projected = jnp.dot(normed_low, in_weight, preferred_element_type=jnp.float32)
        mixed, mix_back = jax.vjp(mixer, projected, conv_weight, conv_bias, dt_bias, a_log, skip_gain, gate_gain)
        mixed_low = mixed.astype(jnp.bfloat16)
        result = (rows_in + jnp.dot(mixed_low, out_weight, preferred_element_type=jnp.float32)).astype(jnp.bfloat16)
        grad_out_w = jnp.dot(mixed_low.T, sequence_grad, preferred_element_type=jnp.float32)
        grad_mixed = jnp.dot(sequence_grad, out_weight.T, preferred_element_type=jnp.float32)
        mix_grads = mix_back(grad_mixed)
        grad_proj_low = mix_grads[0].astype(jnp.bfloat16)
        grad_in_w = jnp.dot(normed_low.T, grad_proj_low, preferred_element_type=jnp.float32)
        grad_normed = jnp.dot(grad_proj_low, in_weight.T, preferred_element_type=jnp.float32)
        grad_rows, grad_norm = norm_back(grad_normed)
        grad_seq = (sequence_grad.astype(jnp.float32) + grad_rows).astype(jnp.bfloat16)
        updates = (grad_in_w, grad_out_w, grad_norm) + tuple(mix_grads[1:])
        new_totals = tuple((total + update for total, update in zip(totals, updates)))
        return (new_totals, (result, grad_seq))
    shapes = (in_weight, out_weight, norm_gain, conv_weight, conv_bias, dt_bias, a_log, skip_gain, gate_gain)
    start_totals = tuple((jnp.zeros(array.shape, jnp.float32) for array in shapes))
    totals, stacked = lax.scan(per_sequence, start_totals, (inputs, cotangent))
    return (stacked[0], stacked[1], totals[2], totals[0], totals[3], totals[4], totals[5], totals[6], totals[7], totals[8], totals[1])
```

```python
import jax
import jax.numpy as jnp
from jax import lax
from jax.experimental import pallas as pl
from jax.experimental.pallas import tpu as pltpu
from jax.sharding import PartitionSpec as P

EPS = 1e-05
LOW = jnp.bfloat16
F32 = jnp.float32
EXACT = lax.Precision.HIGHEST
PAIR = 2


def dot(a, b, dims, precision=None):
    return lax.dot_general(
        a, b, (dims, ((), ())), precision=precision, preferred_element_type=F32
    )


def spread_of(run_col, run_row, length):
    row_ids = lax.broadcasted_iota(jnp.int32, (length, length), 0)
    col_ids = lax.broadcasted_iota(jnp.int32, (length, length), 1)
    return jnp.exp(jnp.where(row_ids >= col_ids, run_col - run_row, -jnp.inf))


def forward_kernel(values, b_ref, c_ref, run_col, run_row, step_row, out, scores):
    length = values.shape[0]
    width = values.shape[1] // PAIR

    @pl.when(pl.program_id(0) == 0)
    def _():
        scores[...] = dot(c_ref[...], b_ref[...], ((1,), (1,)), EXACT)

    parts = []
    for i in range(PAIR):
        decays = spread_of(run_col[0, :, i : i + 1], run_row[0, i : i + 1, :], length)
        weight = scores[...] * (decays * step_row[0, i : i + 1, :])
        vals = values[:, i * width : (i + 1) * width]
        parts.append(dot(weight.astype(LOW), vals.astype(LOW), ((1,), (0,))))
    out[...] = jnp.concatenate(parts, axis=1)


def backward_kernel(
    values, grad, b_ref, c_ref, run_col, run_row, step_row,
    grad_values, row_sums, col_sums, grad_b, grad_c, scores, grad_scores,
):
    length = values.shape[0]
    width = values.shape[1] // PAIR
    at = pl.program_id(0)

    @pl.when(at == 0)
    def _():
        scores[...] = dot(c_ref[...], b_ref[...], ((1,), (1,)), EXACT)
        grad_scores[...] = jnp.zeros_like(grad_scores)

    parts = []
    for i in range(PAIR):
        lanes = slice(i * width, (i + 1) * width)
        step = step_row[0, i : i + 1, :]
        gout = grad[:, lanes]
        grad_weight = dot(gout, values[:, lanes], ((1,), (1,)), EXACT)
        decays = spread_of(run_col[0, :, i : i + 1], run_row[0, i : i + 1, :], length)
        scored = scores[...] * decays
        weight = scored * step
        parts.append(dot(weight.astype(LOW), gout.astype(LOW), ((0,), (0,))))
        terms = grad_weight * scored
        col_sums[0, i : i + 1, :] = jnp.sum(terms, axis=0, keepdims=True)
        row_sums[0, :, i : i + 1] = jnp.sum(terms * step, axis=1, keepdims=True)
        grad_scores[...] += grad_weight * decays * step
    grad_values[...] = jnp.concatenate(parts, axis=1)

    @pl.when(at == pl.num_programs(0) - 1)
    def _():
        total = grad_scores[...]
        grad_c[...] = dot(total, b_ref[...], ((1,), (0,)), EXACT)
        grad_b[...] = dot(total, c_ref[...], ((0,), (0,)), EXACT)


def specs(length, lanes, state, first_b):
    block = pl.BlockSpec((length, lanes), lambda i: (0, i))
    b_spec = pl.BlockSpec((length, state), lambda i: (0, first_b))
    c_spec = pl.BlockSpec((length, state), lambda i: (0, first_b + 1))
    col = pl.BlockSpec((1, length, PAIR), lambda i: (i, 0, 0))
    row = pl.BlockSpec((1, PAIR, length), lambda i: (i, 0, 0))
    return block, b_spec, c_spec, col, row


def as_cols(a):
    length, heads = a.shape
    return a.reshape(length, heads // PAIR, PAIR).transpose(1, 0, 2)


def as_rows(a):
    length, heads = a.shape
    return a.T.reshape(heads // PAIR, PAIR, length)


def shifted(a, by):
    if by == 0:
        return a
    zeros = jnp.zeros((abs(by), a.shape[1]), a.dtype)
    if by > 0:
        return jnp.concatenate([zeros, a[:-by]], axis=0)
    return jnp.concatenate([a[-by:], zeros], axis=0)


def mixer_forward(projected, conv_weight, conv_bias, dt_bias, a_log, skip_gain, gate_gain):
    length = projected.shape[0]
    inner = gate_gain.shape[0]
    heads = skip_gain.shape[0]
    channels = conv_bias.shape[0]
    state = (channels - inner) // 2
    taps = conv_weight.shape[0]
    lanes = inner // heads * PAIR
    gate_in = projected[:, :inner]
    conv_in = projected[:, inner : inner + channels]
    step_in = projected[:, inner + channels :] + dt_bias
    convolved = conv_bias
    for k in range(taps):
        convolved = convolved + conv_weight[k] * shifted(conv_in, taps - 1 - k)
    active = convolved * jax.nn.sigmoid(convolved)
    step = jax.nn.softplus(step_in)
    rate = -jnp.exp(a_log)
    ids = jnp.arange(length)
    lower = (ids[:, None] >= ids[None, :]).astype(F32)
    running = dot(lower, step * rate, ((1,), (0,)), EXACT)
    packed = (as_cols(running), as_rows(running), as_rows(step))
    block, b_spec, c_spec, col, row = specs(length, lanes, state, inner // state)
    scan = pl.pallas_call(
        forward_kernel,
        grid=(heads // PAIR,),
        in_specs=[block, b_spec, c_spec, col, row, row],
        out_specs=block,
        out_shape=jax.ShapeDtypeStruct((length, inner), F32),
        scratch_shapes=[pltpu.VMEM((length, length), F32)],
        cost_estimate=pl.CostEstimate(
            flops=2 * length * length * inner,
            bytes_accessed=8 * length * inner,
            transcendentals=length * length * heads,
        ),
        name="scan_forward",
    )(active, active, active, *packed)
    values = active[:, :inner]
    skip = jnp.repeat(skip_gain, inner // heads)
    scanned = scan + skip * values
    gated = scanned * (gate_in * jax.nn.sigmoid(gate_in))
    scale = lax.rsqrt(jnp.mean(gated * gated, axis=-1, keepdims=True) + EPS)
    mixed = (gated * scale * gate_gain).astype(LOW)
    saved = (gate_in, conv_in, step_in, convolved, active, step, rate, lower, packed, scanned, scale, skip)
    return mixed, saved


def silu_slope(v):
    s = jax.nn.sigmoid(v)
    return s * (1.0 + v * (1.0 - s))


def mixer_backward(saved, grad_mixed, conv_weight, gate_gain):
    gate_in, conv_in, step_in, convolved, active, step, rate, lower, packed, scanned, scale, skip = saved
    length, inner = gate_in.shape
    heads = step.shape[1]
    channels = conv_in.shape[1]
    state = (channels - inner) // 2
    taps = conv_weight.shape[0]
    lanes = inner // heads * PAIR
    silu_gate = gate_in * jax.nn.sigmoid(gate_in)
    gated = scanned * silu_gate
    grad_gain = jnp.sum(grad_mixed * gated * scale, axis=0)
    scaled = grad_mixed * gate_gain
    along = jnp.mean(scaled * gated, axis=-1, keepdims=True)
    grad_gated = scale * scaled - gated * (scale * scale * scale * along)
    grad_gate_in = grad_gated * scanned * silu_slope(gate_in)
    grad_scanned = grad_gated * silu_gate
    values = active[:, :inner]
    grad_skip = jnp.sum(jnp.sum(grad_scanned * values, axis=0).reshape(heads, -1), axis=1)
    block, b_spec, c_spec, col, row = specs(length, lanes, state, inner // state)
    whole = pl.BlockSpec((length, state), lambda i: (0, 0))
    grad_values, row_sums, col_sums, grad_b, grad_c = pl.pallas_call(
        backward_kernel,
        grid=(heads // PAIR,),
        in_specs=[block, block, b_spec, c_spec, col, row, row],
        out_specs=[block, col, row, whole, whole],
        out_shape=[
            jax.ShapeDtypeStruct((length, inner), F32),
            jax.ShapeDtypeStruct((heads // PAIR, length, PAIR), F32),
            jax.ShapeDtypeStruct((heads // PAIR, PAIR, length), F32),
            jax.ShapeDtypeStruct((length, state), F32),
            jax.ShapeDtypeStruct((length, state), F32),
        ],
        scratch_shapes=[pltpu.VMEM((length, length), F32), pltpu.VMEM((length, length), F32)],
        cost_estimate=pl.CostEstimate(
            flops=4 * length * length * inner,
            bytes_accessed=12 * length * inner,
            transcendentals=length * length * heads,
        ),
        name="scan_backward",
    )(active, grad_scanned, active, active, *packed)
    by_row = row_sums.transpose(1, 0, 2).reshape(length, heads)
    by_col = col_sums.reshape(heads, length).T
    grad_running = by_row - by_col * step
    grad_decay = dot(lower, grad_running, ((0,), (0,)), EXACT)
    grad_a_log = jnp.sum(grad_decay * step, axis=0) * rate
    grad_step_in = (by_col + grad_decay * rate) * jax.nn.sigmoid(step_in)
    grad_dt = jnp.sum(grad_step_in, axis=0)
    grad_active = jnp.concatenate([grad_values + grad_scanned * skip, grad_b, grad_c], axis=1)
    grad_conv = grad_active * silu_slope(convolved)
    grad_conv_in = sum(
        conv_weight[k] * shifted(grad_conv, -(taps - 1 - k)) for k in range(taps)
    )
    grad_conv_w = jnp.stack(
        [jnp.sum(grad_conv * shifted(conv_in, taps - 1 - k), axis=0) for k in range(taps)]
    )
    grad_conv_b = jnp.sum(grad_conv, axis=0)
    grad_proj = jnp.concatenate(
        [grad_gate_in.astype(LOW), grad_conv_in.astype(LOW), grad_step_in.astype(LOW)], axis=1
    )
    return grad_proj, (grad_conv_w, grad_conv_b, grad_dt, grad_a_log, grad_skip, grad_gain)


def by_sequence(items):
    return items[0] if len(items) == 1 else jnp.concatenate(items, axis=0)


def reduced(grad_in, grad_out):
    depth, proj = grad_in.shape
    folded = grad_out.astype(LOW).reshape(depth, -1)
    joined = jnp.concatenate([folded, grad_in.astype(LOW)], axis=1)
    half = lax.psum_scatter(joined, ("dp", "rep"), scatter_dimension=0, tiled=True)
    owned = lax.all_gather(half, "rep", axis=0, tiled=True).astype(F32)
    cut = folded.shape[1]
    return owned[:, cut:], owned[:, :cut].reshape(-1, grad_out.shape[1])


def local(
    inputs, norm_gain, in_weight, conv_weight, conv_bias, dt_bias, a_log,
    skip_gain, gate_gain, out_weight, cotangent,
):
    seqs, length, model = inputs.shape
    rows = seqs * length
    in_full = lax.all_gather(in_weight, "dp", axis=0, tiled=True)
    out_full = lax.all_gather(out_weight, "dp", axis=0, tiled=True)
    rows_in = inputs.astype(F32).reshape(rows, model)
    front = lax.rsqrt(jnp.mean(rows_in * rows_in, axis=-1, keepdims=True) + EPS)
    normed = (rows_in * front * norm_gain).astype(LOW)
    projected = dot(normed, in_full, ((1,), (0,)))
    cot = cotangent.reshape(rows, model)

    saved = []
    mixed = []
    for s in range(seqs):
        part, keep = mixer_forward(
            projected[s * length : (s + 1) * length],
            conv_weight, conv_bias, dt_bias, a_log, skip_gain, gate_gain,
        )
        mixed.append(part)
        saved.append(keep)
    mixed = by_sequence(mixed)
    grad_out = dot(mixed, cot, ((0,), (0,)))
    output = (rows_in + dot(mixed, out_full, ((1,), (0,)))).astype(LOW).reshape(inputs.shape)
    grad_mixed = dot(cot, out_full, ((1,), (1,)))

    grad_proj = []
    totals = None
    for s in range(seqs):
        part, sums = mixer_backward(
            saved[s], grad_mixed[s * length : (s + 1) * length], conv_weight, gate_gain
        )
        grad_proj.append(part)
        totals = sums if totals is None else tuple(a + b for a, b in zip(totals, sums))
    grad_proj = by_sequence(grad_proj)
    grad_in, grad_out = reduced(dot(normed, grad_proj, ((0,), (0,))), grad_out)
    grad_normed = dot(grad_proj, in_full, ((1,), (1,)))
    grad_norm = jnp.sum(grad_normed * rows_in * front, axis=0)
    scaled = grad_normed * norm_gain
    along = jnp.mean(scaled * rows_in, axis=-1, keepdims=True)
    grad_rows = front * scaled - rows_in * (front * front * front * along)
    grad_inputs = (cot.astype(F32) + grad_rows).astype(LOW).reshape(inputs.shape)

    smalls = (grad_norm,) + totals
    flat = lax.psum(jnp.concatenate([a.reshape(-1) for a in smalls]), ("dp", "rep"))
    summed = []
    at = 0
    for a in smalls:
        summed.append(flat[at : at + a.size].reshape(a.shape))
        at += a.size
    return (output, grad_inputs, summed[0], grad_in) + tuple(summed[1:]) + (grad_out,)


def solution(mesh):
    rows = P(("dp", "rep"), None, None)
    owned = P("dp", None)
    return jax.shard_map(
        local,
        mesh=mesh,
        in_specs=(rows, P(), owned, P(), P(), P(), P(), P(), P(), owned, rows),
        out_specs=(rows, rows, P(), owned, P(), P(), P(), P(), P(), P(), owned),
        check_vma=False,
    )
```

```python
import jax
import jax.numpy as jnp
from jax import lax
from jax.experimental import pallas as pl
from jax.experimental.pallas import tpu as pltpu
from jax.sharding import PartitionSpec as P

EPS = 1e-05
LOW = jnp.bfloat16
F32 = jnp.float32
EXACT = lax.Precision.HIGHEST
PAIR = 2


def dot(a, b, dims, precision=None):
    return lax.dot_general(
        a, b, (dims, ((), ())), precision=precision, preferred_element_type=F32
    )


def spread_of(run_col, run_row, length):
    row_ids = lax.broadcasted_iota(jnp.int32, (length, length), 0)
    col_ids = lax.broadcasted_iota(jnp.int32, (length, length), 1)
    return jnp.exp(jnp.where(row_ids >= col_ids, run_col - run_row, -jnp.inf))


def forward_kernel(values, b_ref, c_ref, run_col, run_row, step_row, out, scores):
    length = values.shape[0]
    width = values.shape[1] // PAIR

    @pl.when(pl.program_id(0) == 0)
    def _():
        scores[...] = dot(c_ref[...], b_ref[...], ((1,), (1,)), EXACT)

    parts = []
    for i in range(PAIR):
        decays = spread_of(run_col[0, :, i : i + 1], run_row[0, i : i + 1, :], length)
        weight = scores[...] * (decays * step_row[0, i : i + 1, :])
        vals = values[:, i * width : (i + 1) * width]
        parts.append(dot(weight.astype(LOW), vals.astype(LOW), ((1,), (0,))))
    out[...] = jnp.concatenate(parts, axis=1)


def backward_kernel(
    values, grad, b_ref, c_ref, run_col, run_row, step_row,
    grad_values, row_sums, col_sums, grad_b, grad_c, scores, grad_scores,
):
    length = values.shape[0]
    width = values.shape[1] // PAIR
    at = pl.program_id(0)

    @pl.when(at == 0)
    def _():
        scores[...] = dot(c_ref[...], b_ref[...], ((1,), (1,)), EXACT)
        grad_scores[...] = jnp.zeros_like(grad_scores)

    parts = []
    for i in range(PAIR):
        lanes = slice(i * width, (i + 1) * width)
        step = step_row[0, i : i + 1, :]
        gout = grad[:, lanes]
        grad_weight = dot(gout, values[:, lanes], ((1,), (1,)), EXACT)
        decays = spread_of(run_col[0, :, i : i + 1], run_row[0, i : i + 1, :], length)
        scored = scores[...] * decays
        weight = scored * step
        parts.append(dot(weight.astype(LOW), gout.astype(LOW), ((0,), (0,))))
        terms = grad_weight * scored
        col_sums[0, i : i + 1, :] = jnp.sum(terms, axis=0, keepdims=True)
        row_sums[0, :, i : i + 1] = jnp.sum(terms * step, axis=1, keepdims=True)
        grad_scores[...] += grad_weight * decays * step
    grad_values[...] = jnp.concatenate(parts, axis=1)

    @pl.when(at == pl.num_programs(0) - 1)
    def _():
        total = grad_scores[...]
        grad_c[...] = dot(total, b_ref[...], ((1,), (0,)), EXACT)
        grad_b[...] = dot(total, c_ref[...], ((0,), (0,)), EXACT)


def specs(length, lanes, state, first_b):
    block = pl.BlockSpec((length, lanes), lambda i: (0, i))
    b_spec = pl.BlockSpec((length, state), lambda i: (0, first_b))
    c_spec = pl.BlockSpec((length, state), lambda i: (0, first_b + 1))
    col = pl.BlockSpec((1, length, PAIR), lambda i: (i, 0, 0))
    row = pl.BlockSpec((1, PAIR, length), lambda i: (i, 0, 0))
    return block, b_spec, c_spec, col, row


def as_cols(a):
    length, heads = a.shape
    return a.reshape(length, heads // PAIR, PAIR).transpose(1, 0, 2)


def as_rows(a):
    length, heads = a.shape
    return a.T.reshape(heads // PAIR, PAIR, length)


def shifted(a, by):
    if by == 0:
        return a
    zeros = jnp.zeros((abs(by), a.shape[1]), a.dtype)
    if by > 0:
        return jnp.concatenate([zeros, a[:-by]], axis=0)
    return jnp.concatenate([a[-by:], zeros], axis=0)


def mixer_forward(projected, conv_weight, conv_bias, dt_bias, a_log, skip_gain, gate_gain):
    length = projected.shape[0]
    inner = gate_gain.shape[0]
    heads = skip_gain.shape[0]
    channels = conv_bias.shape[0]
    state = (channels - inner) // 2
    taps = conv_weight.shape[0]
    lanes = inner // heads * PAIR
    gate_in = projected[:, :inner]
    conv_in = projected[:, inner : inner + channels]
    step_in = projected[:, inner + channels :] + dt_bias
    convolved = conv_bias
    for k in range(taps):
        convolved = convolved + conv_weight[k] * shifted(conv_in, taps - 1 - k)
    active = convolved * jax.nn.sigmoid(convolved)
    step = jax.nn.softplus(step_in)
    rate = -jnp.exp(a_log)
    ids = jnp.arange(length)
    lower = (ids[:, None] >= ids[None, :]).astype(F32)
    running = dot(lower, step * rate, ((1,), (0,)), EXACT)
    packed = (as_cols(running), as_rows(running), as_rows(step))
    block, b_spec, c_spec, col, row = specs(length, lanes, state, inner // state)
    scan = pl.pallas_call(
        forward_kernel,
        grid=(heads // PAIR,),
        in_specs=[block, b_spec, c_spec, col, row, row],
        out_specs=block,
        out_shape=jax.ShapeDtypeStruct((length, inner), F32),
        scratch_shapes=[pltpu.VMEM((length, length), F32)],
        cost_estimate=pl.CostEstimate(
            flops=2 * length * length * inner,
            bytes_accessed=8 * length * inner,
            transcendentals=length * length * heads,
        ),
        name="scan_forward",
    )(active, active, active, *packed)
    values = active[:, :inner]
    skip = jnp.repeat(skip_gain, inner // heads)
    scanned = scan + skip * values
    gated = scanned * (gate_in * jax.nn.sigmoid(gate_in))
    scale = lax.rsqrt(jnp.mean(gated * gated, axis=-1, keepdims=True) + EPS)
    mixed = (gated * scale * gate_gain).astype(LOW)
    saved = (gate_in, conv_in, step_in, convolved, active, step, rate, lower, packed, scanned, scale, skip)
    return mixed, saved


def silu_slope(v):
    s = jax.nn.sigmoid(v)
    return s * (1.0 + v * (1.0 - s))


def mixer_backward(saved, grad_mixed, conv_weight, gate_gain):
    gate_in, conv_in, step_in, convolved, active, step, rate, lower, packed, scanned, scale, skip = saved
    length, inner = gate_in.shape
    heads = step.shape[1]
    channels = conv_in.shape[1]
    state = (channels - inner) // 2
    taps = conv_weight.shape[0]
    lanes = inner // heads * PAIR
    silu_gate = gate_in * jax.nn.sigmoid(gate_in)
    gated = scanned * silu_gate
    grad_gain = jnp.sum(grad_mixed * gated * scale, axis=0)
    scaled = grad_mixed * gate_gain
    along = jnp.mean(scaled * gated, axis=-1, keepdims=True)
    grad_gated = scale * scaled - gated * (scale * scale * scale * along)
    grad_gate_in = grad_gated * scanned * silu_slope(gate_in)
    grad_scanned = grad_gated * silu_gate
    values = active[:, :inner]
    grad_skip = jnp.sum(jnp.sum(grad_scanned * values, axis=0).reshape(heads, -1), axis=1)
    block, b_spec, c_spec, col, row = specs(length, lanes, state, inner // state)
    whole = pl.BlockSpec((length, state), lambda i: (0, 0))
    grad_values, row_sums, col_sums, grad_b, grad_c = pl.pallas_call(
        backward_kernel,
        grid=(heads // PAIR,),
        in_specs=[block, block, b_spec, c_spec, col, row, row],
        out_specs=[block, col, row, whole, whole],
        out_shape=[
            jax.ShapeDtypeStruct((length, inner), F32),
            jax.ShapeDtypeStruct((heads // PAIR, length, PAIR), F32),
            jax.ShapeDtypeStruct((heads // PAIR, PAIR, length), F32),
            jax.ShapeDtypeStruct((length, state), F32),
            jax.ShapeDtypeStruct((length, state), F32),
        ],
        scratch_shapes=[pltpu.VMEM((length, length), F32), pltpu.VMEM((length, length), F32)],
        cost_estimate=pl.CostEstimate(
            flops=4 * length * length * inner,
            bytes_accessed=12 * length * inner,
            transcendentals=length * length * heads,
        ),
        name="scan_backward",
    )(active, grad_scanned, active, active, *packed)
    by_row = row_sums.transpose(1, 0, 2).reshape(length, heads)
    by_col = col_sums.reshape(heads, length).T
    grad_running = by_row - by_col * step
    grad_decay = dot(lower, grad_running, ((0,), (0,)), EXACT)
    grad_a_log = jnp.sum(grad_decay * step, axis=0) * rate
    grad_step_in = (by_col + grad_decay * rate) * jax.nn.sigmoid(step_in)
    grad_dt = jnp.sum(grad_step_in, axis=0)
    grad_active = jnp.concatenate([grad_values + grad_scanned * skip, grad_b, grad_c], axis=1)
    grad_conv = grad_active * silu_slope(convolved)
    grad_conv_in = sum(
        conv_weight[k] * shifted(grad_conv, -(taps - 1 - k)) for k in range(taps)
    )
    grad_conv_w = jnp.stack(
        [jnp.sum(grad_conv * shifted(conv_in, taps - 1 - k), axis=0) for k in range(taps)]
    )
    grad_conv_b = jnp.sum(grad_conv, axis=0)
    grad_proj = jnp.concatenate(
        [grad_gate_in.astype(LOW), grad_conv_in.astype(LOW), grad_step_in.astype(LOW)], axis=1
    )
    return grad_proj, (grad_conv_w, grad_conv_b, grad_dt, grad_a_log, grad_skip, grad_gain)


def by_sequence(items):
    return items[0] if len(items) == 1 else jnp.concatenate(items, axis=0)


def reduced(grad):
    half = lax.psum_scatter(grad.astype(LOW), ("dp", "rep"), scatter_dimension=0, tiled=True)
    return lax.all_gather(half, "rep", axis=0, tiled=True).astype(F32)


def local(
    inputs, norm_gain, in_weight, conv_weight, conv_bias, dt_bias, a_log,
    skip_gain, gate_gain, out_weight, cotangent,
):
    seqs, length, model = inputs.shape
    rows = seqs * length
    in_full = lax.all_gather(in_weight, "dp", axis=0, tiled=True)
    out_full = lax.all_gather(out_weight, "dp", axis=0, tiled=True)
    rows_in = inputs.astype(F32).reshape(rows, model)
    front = lax.rsqrt(jnp.mean(rows_in * rows_in, axis=-1, keepdims=True) + EPS)
    normed = (rows_in * front * norm_gain).astype(LOW)
    projected = dot(normed, in_full, ((1,), (0,)))
    cot = cotangent.reshape(rows, model)

    saved = []
    mixed = []
    for s in range(seqs):
        part, keep = mixer_forward(
            projected[s * length : (s + 1) * length],
            conv_weight, conv_bias, dt_bias, a_log, skip_gain, gate_gain,
        )
        mixed.append(part)
        saved.append(keep)
    mixed = by_sequence(mixed)
    grad_out = reduced(dot(mixed, cot, ((0,), (0,))))
    output = (rows_in + dot(mixed, out_full, ((1,), (0,)))).astype(LOW).reshape(inputs.shape)
    grad_mixed = dot(cot, out_full, ((1,), (1,)))

    grad_proj = []
    totals = None
    for s in range(seqs):
        part, sums = mixer_backward(
            saved[s], grad_mixed[s * length : (s + 1) * length], conv_weight, gate_gain
        )
        grad_proj.append(part)
        totals = sums if totals is None else tuple(a + b for a, b in zip(totals, sums))
    grad_proj = by_sequence(grad_proj)
    grad_in = reduced(dot(normed, grad_proj, ((0,), (0,))))
    grad_normed = dot(grad_proj, in_full, ((1,), (1,)))
    grad_norm = jnp.sum(grad_normed * rows_in * front, axis=0)
    scaled = grad_normed * norm_gain
    along = jnp.mean(scaled * rows_in, axis=-1, keepdims=True)
    grad_rows = front * scaled - rows_in * (front * front * front * along)
    grad_inputs = (cot.astype(F32) + grad_rows).astype(LOW).reshape(inputs.shape)

    smalls = (grad_norm,) + totals
    flat = lax.psum(jnp.concatenate([a.reshape(-1) for a in smalls]), ("dp", "rep"))
    summed = []
    at = 0
    for a in smalls:
        summed.append(flat[at : at + a.size].reshape(a.shape))
        at += a.size
    return (output, grad_inputs, summed[0], grad_in) + tuple(summed[1:]) + (grad_out,)


def solution(mesh):
    rows = P(("dp", "rep"), None, None)
    owned = P("dp", None)
    return jax.shard_map(
        local,
        mesh=mesh,
        in_specs=(rows, P(), owned, P(), P(), P(), P(), P(), P(), owned, rows),
        out_specs=(rows, rows, P(), owned, P(), P(), P(), P(), P(), P(), owned),
        check_vma=False,
    )
```
